512 devices in a mesh: dp: 16 (over z, core), expert: 32 (over x, y).
Axes of the slice: x: 4, y: 8, z: 8, core: 2. Of those that a mesh axis runs over, the one named last changes fastest.
Arguments:
- layer_input: bfloat16 [1280, 4096], P('expert', 'dp'), may hold values from -6 to 6
- output_grad: bfloat16 [1280, 4096], P('expert', 'dp'), may hold values from -3 to 3
- route_ids: int32 [1280, 8], P('expert'), may hold values from 0 to 31, all different within a row; in each aligned block of 40 rows (0 to 39, 40 to 79, ...) at most 15 rows name the same one
- route_probs: bfloat16 [1280, 8], P('expert'), may hold values from 0.049804688 to 0.3984375
- gate_weight: bfloat16 [32, 4096, 1024], P('expert', 'dp'), may hold values from -0.09375 to 0.09375
- up_weight: bfloat16 [32, 4096, 1024], P('expert', 'dp'), may hold values from -0.09375 to 0.09375
- down_weight: bfloat16 [32, 1024, 4096], P('expert', None, 'dp'), may hold values from -0.1875 to 0.1875
Outputs:
- input_grad: bfloat16 [1280, 4096], P('expert', 'dp')
- prob_grad: bfloat16 [1280, 8], P('expert')
- gate_grad: bfloat16 [32, 4096, 1024], P('expert', 'dp')
- up_grad: bfloat16 [32, 4096, 1024], P('expert', 'dp')
- down_grad: bfloat16 [32, 1024, 4096], P('expert', None, 'dp')
The draws below stay inside these ranges and needn't reach their ends.
Inputs may be any that keep to these rules, and one draw needn't show every extreme that they name: `route_ids`: each token names 8 different experts. In each aligned block of 40 tokens (the tokens of one index of the expert axis) at most 15 tokens name the same expert, and in every draw some expert is named by exactly 15 tokens of some block.
All inputs are finite; a program needn't handle non-finite values.
Results may differ from the reference program's by a relative error of at most 0.035.
Values may be sent and summed in bfloat16 or wider, within the bound.
A program may use at most 64 MiB of HBM per device.

```python
import math
import jax
import jax.numpy as jnp
import numpy as np
from jax import lax

D = 4096
F = 1024
TOK_DEV = 40
EXPERTS = 32
TOPK = 8
CAP = 15
ROWS = 480
TOKENS = 1280
N_DP = 16
N_EXPERT = 32


def block_scale(stream_key, shape, cuts, smallest, high):
    level = 1.0
    for dim, shards_of in cuts:
        draws = jax.random.uniform(jax.random.fold_in(jax.random.fold_in(stream_key, 6), dim), (shards_of,), jnp.float32, smallest / len(cuts), high / len(cuts))
        level = level * jnp.repeat(jnp.exp(draws), shape[dim] // shards_of).reshape((-1,) + (1,) * (len(shape) - 1 - dim))
    return level


def shared_out(rng, own, number, rows, count, top, bound, lean):
    order = jax.random.permutation(rng, count)
    packed, common = load_shares(count, rows * top, bound, lean, True), load_shares(count, rows * top, bound, lean, False)
    places = jnp.arange(count)

    def named(sizes, offset_by):
        used = int((sizes > 0).sum())
        fixed = max(1, used // 4)
        shifted = fixed + (places - fixed + offset_by * (used - fixed)) % max(1, count - fixed)
        return jnp.zeros((count,), jnp.int32).at[order[jnp.where(places < fixed, places, shifted)]].set(jnp.asarray(sizes, jnp.int32))

    sizes = jnp.where(number % 4 == 0, named(packed, number // 4), named(common, number - number // 4 - 1))
    mixed = jax.random.permutation(jax.random.fold_in(own, 3), count)
    donor, sink = mixed[0:count // 2 * 2:2], mixed[1:count // 2 * 2:2]
    margin = jnp.minimum(sizes[donor] - 1, bound - sizes[sink]) // 2
    margin = jnp.where((donor == order[0]) | (sink == order[0]) | (sizes[sink] == 0), 0, jnp.maximum(margin, 0))
    shifted = jax.random.randint(jax.random.fold_in(own, 4), (count // 2,), 0, 1 << 20) % (margin + 1)
    sizes = sizes.at[donor].add(-shifted).at[sink].add(shifted)
    labels = jnp.searchsorted(jnp.cumsum(sizes), jnp.arange(rows * top), side="right").astype(jnp.int32)
    listing = labels.reshape(top, rows).T
    listing = listing[jax.random.permutation(jax.random.fold_in(own, 1), rows)]
    offset_by = jax.random.randint(jax.random.fold_in(own, 2), (rows, 1), 0, top)
    return jnp.take_along_axis(listing, (jnp.arange(top)[None, :] + offset_by) % top, axis=1)


def load_shares(count, total, limit, skew, full):
    loads = [(1 << 20) // math.isqrt(rank ** skew) + 1 for rank in range(1, count + 1)]
    largest = limit if full else min(limit, max(-(-total // count), total * loads[0] // sum(loads)))
    least = 1 if total - largest >= count - 1 else 0
    counts, surplus = [largest] + [least] * (count - 1), total - largest - least * (count - 1)
    while surplus > 0:
        candidates = [i for i in range(1, count) if counts[i] < largest] or [i for i in range(1, count) if counts[i] < limit]
        whole, remaining = sum([loads[i] for i in candidates]), surplus
        for i in candidates:
            extra = min(limit - counts[i], max(1, remaining * loads[i] // whole), surplus)
            counts[i] = counts[i] + extra
            surplus = surplus - extra
    return np.array(counts)


def noise(rng, extent, spread, limit, split=(), held_as=jnp.bfloat16):
    loudness = block_scale(rng, extent, split, -0.22, 0.18) if split else 1.0
    entries = jax.random.normal(rng, extent, jnp.float32) * spread * loudness
    return jnp.minimum(jnp.maximum(entries, -limit), limit).astype(held_as)


def setup_inputs(seed: int = 0) -> dict:
    splits = jax.random.split(jax.random.key(seed), 8)
    layer_input = noise(splits[0], (TOKENS, D), 1.0, 6.0, ((0, 32), (1, 16)))
    output_grad = noise(splits[1], (TOKENS, D), 0.5, 3.0, ((0, 32), (1, 16)))
    route_ids_keys = jax.random.split(jax.random.fold_in(splits[2], 1), TOKENS // TOK_DEV)
    route_ids_turns = jax.random.permutation(jax.random.fold_in(splits[2], 3), TOKENS // TOK_DEV)
    route_ids = jax.vmap(lambda own, number: shared_out(jax.random.fold_in(splits[2], 2), own, number, TOK_DEV, EXPERTS, TOPK, CAP, 2))(route_ids_keys, route_ids_turns).reshape((TOKENS, TOPK))
    route_probs = jnp.clip(0.049804688 + 0.3486328 * jax.random.uniform(splits[3], (TOKENS, TOPK), jnp.float32) ** block_scale(splits[3], (TOKENS, TOPK), ((0, 32),), -0.2, 0.2), 0.049804688, 0.3984375).astype(jnp.bfloat16)
    gate_weight = noise(splits[4], (EXPERTS, D, F), D ** -0.5, 0.09375, ((0, 32), (1, 16)))
    up_weight = noise(splits[5], (EXPERTS, D, F), D ** -0.5, 0.09375, ((0, 32), (1, 16)))
    down_weight = noise(splits[6], (EXPERTS, F, D), F ** -0.5, 0.1875, ((0, 32), (2, 16)))
    return dict(layer_input=layer_input, output_grad=output_grad, route_ids=route_ids, route_probs=route_probs, gate_weight=gate_weight, up_weight=up_weight, down_weight=down_weight)


def swiglu_back(gate_pre, up_pre, hidden_grad):
    sig_gate = jax.nn.sigmoid(gate_pre)
    active = (gate_pre * sig_gate * up_pre).astype(jnp.bfloat16)
    gate_delta = (hidden_grad * up_pre * sig_gate * (1.0 + gate_pre * (1.0 - sig_gate))).astype(jnp.bfloat16)
    up_delta = (hidden_grad * gate_pre * sig_gate).astype(jnp.bfloat16)
    return active, gate_delta, up_delta


def block_sum(left, right):
    width_part = D // N_DP
    partials = jnp.einsum('rnd,ndf->nrf', left.astype(jnp.float32).reshape(ROWS, N_DP, width_part),
                          right.astype(jnp.float32).reshape(N_DP, width_part, right.shape[1]))
    rounded = lax.optimization_barrier(partials.astype(jnp.bfloat16))
    return jnp.sum(rounded.astype(jnp.float32), axis=0)


def reference(layer_input, output_grad, route_ids, route_probs, gate_weight, up_weight, down_weight):
    onehot = (route_ids[:, :, None] == jnp.arange(EXPERTS, dtype=jnp.int32)).astype(jnp.int32)
    member = jnp.sum(onehot, axis=1)
    member_b = member.reshape(N_EXPERT, TOK_DEV, EXPERTS)
    before = jnp.cumsum(member_b, axis=1) - member_b
    pweight = jnp.sum(onehot.astype(jnp.float32) * route_probs.astype(jnp.float32)[:, :, None], axis=1)
    pweight = pweight.reshape(N_EXPERT, TOK_DEV, EXPERTS)
    input_b = layer_input.astype(jnp.float32).reshape(N_EXPERT, TOK_DEV, D)
    grad_b = output_grad.astype(jnp.float32).reshape(N_EXPERT, TOK_DEV, D)
    cslots = jnp.arange(CAP, dtype=jnp.int32)

    def expert_pass(expert):
        mem = jnp.take(member_b, expert, axis=2)
        bef = jnp.take(before, expert, axis=2)
        pwe = jnp.take(pweight, expert, axis=2)
        select = ((bef[:, :, None] == cslots) & (mem[:, :, None] > 0)).astype(jnp.float32)
        rows_x = jnp.einsum('stc,std->scd', select, input_b).reshape(ROWS, D).astype(jnp.bfloat16)
        rows_g = jnp.einsum('stc,std->scd', select, grad_b).reshape(ROWS, D).astype(jnp.bfloat16)
        rows_p = jnp.einsum('stc,st->sc', select, pwe).reshape(ROWS).astype(jnp.bfloat16)
        gate_w = gate_weight[expert]
        up_w = up_weight[expert]
        down_w = down_weight[expert]
        scaled = (rows_p.astype(jnp.float32)[:, None] * rows_g.astype(jnp.float32)).astype(jnp.bfloat16)
        gate_pre = block_sum(rows_x, gate_w)
        up_pre = block_sum(rows_x, up_w)
        hidden_grad = block_sum(scaled, down_w.T)
        active, gate_delta, up_delta = swiglu_back(gate_pre, up_pre, hidden_grad)
        out_rows = jnp.dot(active.astype(jnp.float32), down_w.astype(jnp.float32))
        gate_dot = jnp.sum(rows_g.astype(jnp.float32) * out_rows, axis=1).astype(jnp.bfloat16)
        down_g = jnp.dot(active.astype(jnp.float32).T, scaled.astype(jnp.float32)).astype(jnp.bfloat16)
        gate_g = jnp.dot(rows_x.astype(jnp.float32).T, gate_delta.astype(jnp.float32)).astype(jnp.bfloat16)
        up_g = jnp.dot(rows_x.astype(jnp.float32).T, up_delta.astype(jnp.float32)).astype(jnp.bfloat16)
        row_grad = (jnp.dot(gate_delta.astype(jnp.float32), gate_w.astype(jnp.float32).T)
                    + jnp.dot(up_delta.astype(jnp.float32), up_w.astype(jnp.float32).T)).astype(jnp.bfloat16)
        return row_grad, gate_dot, gate_g, up_g, down_g

    row_all, dot_all, gate_grad, up_grad, down_grad = lax.map(expert_pass, jnp.arange(EXPERTS, dtype=jnp.int32))
    before_flat = before.reshape(TOKENS, EXPERTS)
    slot_k = jnp.sum(onehot * before_flat[:, None, :], axis=2).astype(jnp.int32)
    source = (jnp.arange(TOKENS, dtype=jnp.int32) // TOK_DEV).astype(jnp.int32)
    row_index = (route_ids * ROWS + source[:, None] * CAP + slot_k).astype(jnp.int32)
    picked = jnp.take(row_all.reshape(EXPERTS * ROWS, D), row_index.reshape(-1), axis=0)
    picked = picked.reshape(TOKENS, TOPK, D).astype(jnp.float32)
    input_grad = jnp.sum(picked, axis=1).astype(jnp.bfloat16)
    prob_grad = jnp.take(dot_all.reshape(-1), row_index.reshape(-1)).reshape(TOKENS, TOPK)
    return input_grad, prob_grad, gate_grad, up_grad, down_grad
```

```python
import functools

import jax
import jax.numpy as jnp
from jax import lax
from jax.experimental import pallas as pl
from jax.experimental.pallas import tpu as pltpu
from jax.sharding import PartitionSpec as P

MESH = pl.DeviceIdType.MESH
BF = jnp.bfloat16
F32 = jnp.float32
BLK = 16
LANE = 128


def log2(n):
    return n.bit_length() - 1


def dot(a, b, ca=1, cb=0):
    return lax.dot_general(a, b, (((ca,), (cb,)), ((), ())), preferred_element_type=F32)


def iota(shape, dim):
    return lax.broadcasted_iota(jnp.int32, shape, dim)


def split_rows(block, width):
    rows = block.shape[0]
    x = block[:, :width].astype(F32)
    g = block[:, width:]
    head = x[:, :LANE].reshape(rows // BLK, BLK, LANE)
    shape = head.shape
    diag = iota(shape, 1) == iota(shape, 2)
    spread = jnp.broadcast_to(head[:, BLK - 1 :, :], shape)
    col = jnp.sum(jnp.where(diag, spread, 0.0), axis=2, keepdims=True).reshape(rows, 1)
    keep = (iota(x.shape, 0) & (BLK - 1)) != BLK - 1
    return jnp.where(keep, x, 0.0).astype(BF), g, col


def kernel(
    nx, ny, nz,
    x_ref, g_ref, ids_ref, prob_ref, gw_ref, uw_ref, dw_ref,
    xgrad_ref, pgrad_ref, ggrad_ref, ugrad_ref, dgrad_ref,
    tok, sel, send, recv, peer, part, rs_in, rs_out, hid, rgrad, back, pgw, puw, pdw, pcol, member_s,
    disp_s, disp_r, ret_s, ret_r, w_s, w_r, fwd_s, fwd_r, rs_s, rs_r, ag_s, ag_r, pt_s, pt_r,
):
    toks, width = x_ref.shape
    topk = ids_ref.shape[1]
    slots = nx * ny
    rows = slots * BLK
    chunks = ny // 2
    half = nx * BLK
    crows = 2 * half
    per = 2 * nx
    ha, hb = nz // 2, nz // 2 - 1
    lx = log2(nx)

    dp = lax.axis_index("dp")
    ex = lax.axis_index("expert")
    z, core = dp // 2, dp % 2
    mx, my = ex // ny, ex % ny
    s = 1 - 2 * core

    def zdev(step):
        return {"dp": ((z + step * s + nz) % nz) * 2 + core}

    fore, aft = zdev(1), zdev(-1)
    other = {"dp": z * 2 + 1 - core}

    def offset(q):
        c, b, dx = q // per, (q // nx) % 2, q % nx
        dy = jnp.where(b == 0, -c, c + 1)
        return dx, dy

    def target(q):
        dx, dy = offset(q)
        return {"expert": ((mx + dx) % nx) * ny + (my + dy + ny) % ny}

    def origin(q):
        dx, dy = offset(q)
        return {"expert": ((mx - dx + nx) % nx) * ny + (my - dy + ny) % ny}

    def remote(src, dst, ssem, rsem, dev):
        return pltpu.make_async_remote_copy(
            src_ref=src, dst_ref=dst, send_sem=ssem, recv_sem=rsem, device_id=dev, device_id_type=MESH
        )

    barrier = pltpu.get_barrier_semaphore()

    @pl.loop(1, slots)
    def _(q):
        pl.semaphore_signal(barrier, inc=1, device_id=target(q), device_id_type=MESH)

    for dev in (fore, aft, other):
        pl.semaphore_signal(barrier, inc=1, device_id=dev, device_id_type=MESH)

    q_lane = iota((toks, slots), 1)
    c_l, b_l, dx_l = q_lane >> (lx + 1), (q_lane >> lx) & 1, q_lane & (nx - 1)
    dy_l = jnp.where(b_l == 0, -c_l, c_l + 1)
    named = ((mx + dx_l) & (nx - 1)) * ny + ((my + dy_l) & (ny - 1))
    ids = ids_ref[...]
    prob = prob_ref[...].astype(F32)
    member = jnp.zeros((toks, slots), F32)
    weight = jnp.zeros((toks, slots), F32)
    for k in range(topk):
        hit = ids[:, k : k + 1] == named
        member = member + jnp.where(hit, 1.0, 0.0)
        weight = weight + jnp.where(hit, prob[:, k : k + 1], 0.0)
    lower = jnp.where(iota((toks, toks), 1) < iota((toks, toks), 0), 1.0, 0.0).astype(BF)
    before = dot(lower, member.astype(BF))
    slot = jnp.where(member > 0.0, before, -1.0)
    own_lane = (iota((slots, rows), 1) >> 4) == iota((slots, rows), 0)
    expand = jnp.where(own_lane, 1.0, 0.0).astype(BF)
    slot_x = dot(slot.astype(BF), expand)
    lane16 = (iota((toks, rows), 1) & (BLK - 1)).astype(F32)
    chosen = slot_x == lane16
    weight_x = dot(weight.astype(BF), expand)
    prob_vec = jnp.sum(jnp.where(chosen, weight_x, 0.0), axis=0, keepdims=True)
    spread = jnp.where((iota((rows, LANE), 0) & (BLK - 1)) == iota((rows, LANE), 1), 1.0, 0.0).astype(BF)
    prob_rows = dot(jnp.where(own_lane, prob_vec, 0.0).astype(BF), spread)
    scalar_lane = iota((slots, rows), 1) == iota((slots, rows), 0) * BLK + (BLK - 1)
    sel[0:slots, :] = jnp.where(scalar_lane, 1.0, 0.0).astype(BF)
    sel[slots : slots + toks, :] = jnp.where(chosen, 1.0, 0.0).astype(BF)
    tok[0:slots, :] = jnp.zeros((slots, 2 * width), BF)
    tok[0:slots, 0:LANE] = prob_rows.astype(BF)
    tok[slots : slots + toks, 0:width] = x_ref[...]
    tok[slots : slots + toks, width : 2 * width] = g_ref[...]
    packed = dot(sel[...], tok[...], 0, 0).astype(BF)
    send[...] = packed
    recv[0:BLK, :] = packed[0:BLK]

    pl.semaphore_wait(barrier, slots - 1 + 3)

    def w_copy(i):
        src, dst = ((gw_ref, pgw), (uw_ref, puw), (dw_ref, pdw))[i]
        return remote(src, dst, w_s.at[i], w_r.at[i], other)

    def block(q):
        return pl.ds(pl.multiple_of(q * BLK, BLK), BLK)

    def disp_copy(q):
        return remote(send.at[block(q)], recv.at[block(q)], disp_s.at[q], disp_r.at[q], target(q))

    def ret_copy(q):
        return remote(rgrad.at[block(q)], back.at[block(q)], ret_s.at[q], ret_r.at[q], origin(q))

    for i in range(3):
        w_copy(i).start()

    @pl.loop(1, slots)
    def _(q):
        disp_copy(q).start()

    def half_rows(k, h):
        return pl.ds(pl.multiple_of(k * crows + h * half, BLK), half)

    def fwd_copy(k):
        return remote(recv.at[half_rows(k, 1 - core)], peer.at[k], fwd_s.at[k], fwd_r.at[k], other)

    def zcol(step):
        j = (z + step * s + nz) % nz
        return j, pl.ds(pl.multiple_of(j * LANE, LANE), LANE)

    def rs_copy(k, i):
        return remote(rs_out.at[k, i], rs_in.at[k, i], rs_s.at[k, i], rs_r.at[k, i], fore if i < ha else aft)

    def rs_hop(k, h):
        for i, step, hops in ((h, ha - h, ha), (ha + h, h - hb, hb)):
            if h >= hops:
                continue
            v = part[k, :, :, zcol(step)[1]]
            if h > 0:
                rs_copy(k, i - 1).wait_recv()
                v = v + rs_in[k, i - 1].astype(F32)
            rs_out[k, i] = v.astype(BF)
            rs_copy(k, i).start()

    def hid_at(k, step):
        return hid.at[:, half_rows(k, core), zcol(step)[1]]

    def ag_copy(k, i):
        if i < ha:
            return remote(hid_at(k, -i), hid_at(k, -i), ag_s.at[k, i], ag_r.at[k, i], fore)
        return remote(hid_at(k, i - ha), hid_at(k, i - ha), ag_s.at[k, i], ag_r.at[k, i], aft)

    def pt_copy(k, step):
        j, _ = zcol(step)
        return remote(hid_at(k, step), hid_at(k, step), pt_s.at[k, j], pt_r.at[k, j], other)

    def arrive(k):
        @pl.loop(max(1, k * per), (k + 1) * per)
        def _(q):
            disp_copy(q).wait_recv()

        fwd_copy(k).start()

    def partials(k):
        fwd_copy(k).wait_recv()
        if k == 0:
            for i in range(3):
                w_copy(i).wait_recv()
        x0, g0, col = split_rows(recv[half_rows(k, core), :], width)
        x1, g1, _ = split_rows(peer[k], width)
        pcol[k] = jnp.broadcast_to(col, (half, LANE))
        part[k, 0] = dot(x0, gw_ref[...]) + dot(x1, pgw[...])
        part[k, 1] = dot(x0, uw_ref[...]) + dot(x1, puw[...])
        part[k, 2] = dot(g0, dw_ref[...], 1, 1) + dot(g1, pdw[...], 1, 1)
        rs_hop(k, 0)

    def swiglu(k):
        rs_copy(k, ha - 1).wait_recv()
        v = part[k, :, :, zcol(0)[1]] + rs_in[k, ha - 1].astype(F32)
        if hb > 0:
            rs_copy(k, ha + hb - 1).wait_recv()
            v = v + rs_in[k, ha + hb - 1].astype(F32)
        gate_pre, up_pre, raw = v[0], v[1], v[2]
        hidden_grad = raw * pcol[k]
        sig = 1.0 / (1.0 + jnp.exp(-gate_pre))
        active = gate_pre * sig * up_pre
        gate_delta = hidden_grad * up_pre * sig * (1.0 + gate_pre * (1.0 - sig))
        up_delta = hidden_grad * gate_pre * sig
        inner = jnp.sum(active * raw, axis=1, keepdims=True)
        shape = (half // BLK, BLK, LANE)
        diag = iota(shape, 1) == iota(shape, 2)
        spread = jnp.broadcast_to(inner, (half, LANE)).reshape(shape)
        line = jnp.sum(jnp.where(diag, spread, 0.0), axis=1, keepdims=True)
        high = line.astype(BF).astype(F32)
        last = iota(shape, 1) == BLK - 1

        def with_line(body, extra):
            return jnp.where(last, extra, body.reshape(shape)).reshape(half, LANE).astype(BF)

        at = (half_rows(k, core), zcol(0)[1])
        hid[(0, *at)] = with_line(active, high)
        hid[(1, *at)] = with_line(gate_delta, line - high)
        hid[(2, *at)] = up_delta.astype(BF)
        ag_copy(k, 0).start()
        if hb > 0:
            ag_copy(k, ha).start()
        pt_copy(k, 0).start()

    def ag_hop(k, h):
        for i, step, hops in ((h, -(h + 1), ha), (ha + h, h + 1, hb)):
            if h >= hops:
                continue
            ag_copy(k, i).wait_recv()
            if h + 1 < hops:
                ag_copy(k, i + 1).start()
            pt_copy(k, step).start()

    def give_back(k):
        for j in range(nz):
            at = hid.at[:, half_rows(k, 1 - core), pl.ds(j * LANE, LANE)]
            remote(at, at, pt_s.at[k, j], pt_r.at[k, j], other).wait_recv()
        mine = pl.ds(k * crows, crows)
        grad = dot(hid[1, mine, :], gw_ref[...], 1, 1) + dot(hid[2, mine, :], uw_ref[...], 1, 1)
        line = hid[0, mine, 0:LANE].astype(F32) + hid[1, mine, 0:LANE].astype(F32)
        for j in range(1, nz):
            at = slice(j * LANE, (j + 1) * LANE)
            line = line + hid[0, mine, at].astype(F32) + hid[1, mine, at].astype(F32)
        wide = jnp.concatenate([line] + [jnp.zeros_like(line)] * (width // LANE - 1), axis=1)
        last = (iota((crows, width), 0) & (BLK - 1)) == BLK - 1
        out = jnp.where(last, wide, grad).astype(BF)
        rgrad[mine, :] = out
        if k == 0:
            back[0:BLK, :] = out[0:BLK]

        @pl.loop(max(1, k * per), (k + 1) * per)
        def _(q):
            ret_copy(q).start()

    stages = [arrive, partials]
    stages += [functools.partial(lambda k, h: rs_hop(k, h), h=h) for h in range(1, ha)]
    stages += [swiglu]
    stages += [functools.partial(lambda k, h: ag_hop(k, h), h=h) for h in range(ha)]
    stages += [give_back]
    for tick in range(len(stages) + chunks - 1):
        for k in range(chunks):
            if 0 <= tick - k < len(stages):
                stages[tick - k](k)

    xs, gs, col = split_rows(recv[...], width)
    scaled = (gs.astype(F32) * col).astype(BF)
    ggrad_ref[...] = dot(xs, hid[1], 0, 0).astype(BF)
    ugrad_ref[...] = dot(xs, hid[2], 0, 0).astype(BF)
    dgrad_ref[...] = dot(hid[0], scaled, 0, 0).astype(BF)

    @pl.loop(1, slots)
    def _(q):
        ret_copy(q).wait_recv()

    picks = sel[slots : slots + toks, :]
    xgrad_ref[...] = dot(picks, back[...]).astype(BF)
    lines = back[...].astype(F32).reshape(slots, BLK, width)[:, BLK - 1, 0:LANE].astype(BF)
    line_x = jnp.where(own_lane, dot(lines, spread, 1, 1), 0.0)
    line_vec = jnp.sum(line_x, axis=0, keepdims=True)
    table = dot((picks.astype(F32) * line_vec).astype(BF), expand, 1, 1)
    result = jnp.zeros((toks, topk), F32)
    k_lane = iota((toks, topk), 1)
    for k in range(topk):
        hit = ids[:, k : k + 1] == named
        value = jnp.sum(jnp.where(hit, table, 0.0), axis=1, keepdims=True)
        result = jnp.where(k_lane == k, value, result)
    pgrad_ref[...] = result.astype(BF)

    for i in range(3):
        w_copy(i).wait_send()

    @pl.loop(1, slots)
    def _(q):
        disp_copy(q).wait_send()
        ret_copy(q).wait_send()

    for k in range(chunks):
        fwd_copy(k).wait_send()
        for i in range(ha + hb):
            rs_copy(k, i).wait_send()
            ag_copy(k, i).wait_send()
        for j in range(nz):
            at = hid.at[:, half_rows(k, core), pl.ds(j * LANE, LANE)]
            remote(at, at, pt_s.at[k, j], pt_r.at[k, j], other).wait_send()


def on_device(sizes, layer_input, output_grad, route_ids, route_probs, gate_weight, up_weight, down_weight):
    nx, ny, nz = sizes
    toks, width = layer_input.shape
    hidden = gate_weight.shape[2]
    topk = route_ids.shape[1]
    slots = nx * ny
    rows = slots * BLK
    chunks = ny // 2
    half = nx * BLK
    hops = nz - 1
    assert hidden == nz * LANE
    assert 3 * toks * topk // (2 * slots) < BLK
    vmem = pl.BlockSpec(memory_space=pltpu.VMEM)
    dma = pltpu.SemaphoreType.DMA
    outs = pl.pallas_call(
        functools.partial(kernel, nx, ny, nz),
        out_shape=(
            jax.ShapeDtypeStruct((toks, width), BF),
            jax.ShapeDtypeStruct((toks, topk), BF),
            jax.ShapeDtypeStruct((width, hidden), BF),
            jax.ShapeDtypeStruct((width, hidden), BF),
            jax.ShapeDtypeStruct((hidden, width), BF),
        ),
        in_specs=[vmem] * 7,
        out_specs=[vmem] * 5,
        scratch_shapes=[
            pltpu.VMEM((slots + toks, 2 * width), BF),
            pltpu.VMEM((slots + toks, rows), BF),
            pltpu.VMEM((rows, 2 * width), BF),
            pltpu.VMEM((rows, 2 * width), BF),
            pltpu.VMEM((chunks, half, 2 * width), BF),
            pltpu.VMEM((chunks, 3, half, hidden), F32),
            pltpu.VMEM((chunks, hops, 3, half, LANE), BF),
            pltpu.VMEM((chunks, hops, 3, half, LANE), BF),
            pltpu.VMEM((3, rows, hidden), BF),
            pltpu.VMEM((rows, width), BF),
            pltpu.VMEM((rows, width), BF),
            pltpu.VMEM((width, hidden), BF),
            pltpu.VMEM((width, hidden), BF),
            pltpu.VMEM((hidden, width), BF),
            pltpu.VMEM((chunks, half, LANE), F32),
            pltpu.VMEM((8, LANE), F32),
            dma((slots,)), dma((slots,)), dma((slots,)), dma((slots,)),
            dma((3,)), dma((3,)),
            dma((chunks,)), dma((chunks,)),
            dma((chunks, hops)), dma((chunks, hops)),
            dma((chunks, hops)), dma((chunks, hops)),
            dma((chunks, nz)), dma((chunks, nz)),
        ],
        compiler_params=pltpu.CompilerParams(
            collective_id=0, has_side_effects=True, vmem_limit_bytes=60 * 1024 * 1024
        ),
    )(
        layer_input, output_grad, route_ids, route_probs,
        gate_weight[0], up_weight[0], down_weight[0],
    )
    xgrad, pgrad, ggrad, ugrad, dgrad = outs
    return (xgrad, pgrad, ggrad[None], ugrad[None], dgrad[None])


def solution(mesh, sizes=(4, 8, 8)):
    placed = (
        P("expert", "dp"),
        P("expert", "dp"),
        P("expert", None),
        P("expert", None),
        P("expert", "dp", None),
        P("expert", "dp", None),
        P("expert", None, "dp"),
    )
    return jax.shard_map(
        functools.partial(on_device, sizes),
        mesh=mesh,
        in_specs=placed,
        out_specs=(
            P("expert", "dp"),
            P("expert", None),
            P("expert", "dp", None),
            P("expert", "dp", None),
            P("expert", None, "dp"),
        ),
        check_vma=False,
    )
```

```python
import functools

import jax
import jax.numpy as jnp
from jax import lax
from jax.experimental import pallas as pl
from jax.experimental.pallas import tpu as pltpu
from jax.sharding import PartitionSpec as P

MESH = pl.DeviceIdType.MESH
BF = jnp.bfloat16
F32 = jnp.float32
BLK = 16
LANE = 128
PLAN = (
    (0, 0), (1, 0), (0, 1), (2, 0), (1, 1), (3, 0), (0, 2), (4, 0), (2, 1), (1, 2), (5, 0), (3, 1), (2, 2), (0, 3),
    (6, 0), (1, 3), (4, 1), (3, 2), (2, 3), (7, 0), (5, 1), (4, 2), (3, 3), (8, 0), (6, 1), (5, 2), (4, 3),
    (9, 0), (7, 1), (6, 2), (5, 3), (8, 1), (7, 2), (6, 3), (10, 0), (9, 1), (8, 2), (7, 3), (10, 1), (9, 2), (8, 3),
    (10, 2), (9, 3), (10, 3),
)


def log2(n):
    return n.bit_length() - 1


def dot(a, b, ca=1, cb=0):
    return lax.dot_general(a, b, (((ca,), (cb,)), ((), ())), preferred_element_type=F32)


def iota(shape, dim):
    return lax.broadcasted_iota(jnp.int32, shape, dim)


def split_rows(block, width):
    rows = block.shape[0]
    x = block[:, :width].astype(F32)
    g = block[:, width:]
    head = x[:, :LANE].reshape(rows // BLK, BLK, LANE)
    shape = head.shape
    diag = iota(shape, 1) == iota(shape, 2)
    spread = jnp.broadcast_to(head[:, BLK - 1 :, :], shape)
    col = jnp.sum(jnp.where(diag, spread, 0.0), axis=2, keepdims=True).reshape(rows, 1)
    keep = (iota(x.shape, 0) & (BLK - 1)) != BLK - 1
    return jnp.where(keep, x, 0.0).astype(BF), g, col


def kernel(
    nx, ny, nz,
    x_ref, g_ref, ids_ref, prob_ref, gate_hbm, up_hbm, down_hbm,
    xgrad_ref, pgrad_ref, ggrad_hbm, ugrad_hbm, dgrad_hbm,
    tok, sel, send, recv, peer, part, rs_in, rs_out, hid, rgrad, back, pgw, puw, pdw, pcol,
    gw_ref, uw_ref, dw_ref, ggrad_ref, ugrad_ref, dgrad_ref, in_s, out_s,
    disp_s, disp_r, ret_s, ret_r, w_s, w_r, fwd_s, fwd_r, rs_s, rs_r, ag_s, ag_r, pt_s, pt_r,
):
    toks, width = x_ref.shape
    topk = ids_ref.shape[0]
    slots = nx * ny
    rows = slots * BLK
    chunks = ny // 2
    half = nx * BLK
    crows = 2 * half
    per = 2 * nx
    ha, hb = nz // 2, nz // 2 - 1
    lx = log2(nx)

    dp = lax.axis_index("dp")
    ex = lax.axis_index("expert")
    z, core = dp // 2, dp % 2
    mx, my = ex // ny, ex % ny
    s = 1 - 2 * core

    def zdev(step):
        return {"dp": ((z + step * s + nz) % nz) * 2 + core}

    fore, aft = zdev(1), zdev(-1)
    other = {"dp": z * 2 + 1 - core}

    def offset(q):
        c, b, dx = q // per, (q // nx) % 2, q % nx
        dy = jnp.where(b == 0, -c, c + 1)
        return dx, dy

    def target(q):
        dx, dy = offset(q)
        return {"expert": ((mx + dx) % nx) * ny + (my + dy + ny) % ny}

    def origin(q):
        dx, dy = offset(q)
        return {"expert": ((mx - dx + nx) % nx) * ny + (my - dy + ny) % ny}

    def remote(src, dst, ssem, rsem, dev):
        return pltpu.make_async_remote_copy(
            src_ref=src, dst_ref=dst, send_sem=ssem, recv_sem=rsem, device_id=dev, device_id_type=MESH
        )

    loads = ((gate_hbm, gw_ref), (up_hbm, uw_ref), (down_hbm, dw_ref))
    stores = ((ggrad_ref, ggrad_hbm), (ugrad_ref, ugrad_hbm), (dgrad_ref, dgrad_hbm))

    def load(i):
        return pltpu.make_async_copy(*loads[i], in_s.at[i])

    def store(i):
        return pltpu.make_async_copy(*stores[i], out_s.at[i])

    barrier = pltpu.get_barrier_semaphore()

    @pl.loop(1, slots)
    def _(q):
        pl.semaphore_signal(barrier, inc=1, device_id=target(q), device_id_type=MESH)

    for dev in (fore, aft, other):
        pl.semaphore_signal(barrier, inc=1, device_id=dev, device_id_type=MESH)

    for i in range(3):
        load(i).start()

    q_lane = iota((toks, slots), 1)
    c_l, b_l, dx_l = q_lane >> (lx + 1), (q_lane >> lx) & 1, q_lane & (nx - 1)
    dy_l = jnp.where(b_l == 0, -c_l, c_l + 1)
    named = (((mx + dx_l) & (nx - 1)) * ny + ((my + dy_l) & (ny - 1))).astype(F32)
    eye = jnp.where(iota((toks, toks), 0) == iota((toks, toks), 1), 1.0, 0.0).astype(BF)
    ids = dot(eye, ids_ref[...].astype(F32).astype(BF), 1, 1)
    prob = dot(eye, prob_ref[...], 1, 1)
    member = jnp.zeros((toks, slots), F32)
    weight = jnp.zeros((toks, slots), F32)
    for k in range(topk):
        hit = ids[:, k : k + 1] == named
        member = member + jnp.where(hit, 1.0, 0.0)
        weight = weight + jnp.where(hit, prob[:, k : k + 1], 0.0)
    lower = jnp.where(iota((toks, toks), 1) < iota((toks, toks), 0), 1.0, 0.0).astype(BF)
    before = dot(lower, member.astype(BF))
    slot = jnp.where(member > 0.0, before, -1.0)
    own_lane = (iota((slots, rows), 1) >> 4) == iota((slots, rows), 0)
    expand = jnp.where(own_lane, 1.0, 0.0).astype(BF)
    slot_x = dot(slot.astype(BF), expand)
    lane16 = (iota((toks, rows), 1) & (BLK - 1)).astype(F32)
    chosen = slot_x == lane16
    weight_x = dot(weight.astype(BF), expand)
    prob_vec = jnp.sum(jnp.where(chosen, weight_x, 0.0), axis=0, keepdims=True)
    spread = jnp.where((iota((rows, LANE), 0) & (BLK - 1)) == iota((rows, LANE), 1), 1.0, 0.0).astype(BF)
    prob_rows = dot(jnp.where(own_lane, prob_vec, 0.0).astype(BF), spread)
    scalar_lane = iota((slots, rows), 1) == iota((slots, rows), 0) * BLK + (BLK - 1)
    sel[0:slots, :] = jnp.where(scalar_lane, 1.0, 0.0).astype(BF)
    sel[slots : slots + toks, :] = jnp.where(chosen, 1.0, 0.0).astype(BF)
    tok[0:slots, :] = jnp.zeros((slots, 2 * width), BF)
    tok[0:slots, 0:LANE] = prob_rows.astype(BF)
    tok[slots : slots + toks, 0:width] = x_ref[...]
    tok[slots : slots + toks, width : 2 * width] = g_ref[...]
    packed = dot(sel[...], tok[...], 0, 0).astype(BF)
    send[...] = packed
    recv[0:BLK, :] = packed[0:BLK]

    pl.semaphore_wait(barrier, slots - 1 + 3)

    def w_copy(i):
        src, dst = ((gate_hbm, pgw), (up_hbm, puw), (down_hbm, pdw))[i]
        return remote(src, dst, w_s.at[i], w_r.at[i], other)

    def block(q):
        return pl.ds(pl.multiple_of(q * BLK, BLK), BLK)

    def disp_copy(q):
        return remote(send.at[block(q)], recv.at[block(q)], disp_s.at[q], disp_r.at[q], target(q))

    def ret_copy(q):
        return remote(rgrad.at[block(q)], back.at[block(q)], ret_s.at[q], ret_r.at[q], origin(q))

    for i in range(3):
        w_copy(i).start()

    @pl.loop(1, slots)
    def _(q):
        disp_copy(q).start()

    def half_rows(k, h):
        return pl.ds(pl.multiple_of(k * crows + h * half, BLK), half)

    def fwd_copy(k):
        return remote(recv.at[half_rows(k, 1 - core)], peer.at[k], fwd_s.at[k], fwd_r.at[k], other)

    def zcol(step):
        j = (z + step * s + nz) % nz
        return j, pl.ds(pl.multiple_of(j * LANE, LANE), LANE)

    def rs_copy(k, i):
        return remote(rs_out.at[k, i], rs_in.at[k, i], rs_s.at[k, i], rs_r.at[k, i], fore if i < ha else aft)

    def rs_hop(k, h):
        for i, step, hops in ((h, ha - h, ha), (ha + h, h - hb, hb)):
            if h >= hops:
                continue
            v = part[k, :, :, zcol(step)[1]]
            if h > 0:
                rs_copy(k, i - 1).wait_recv()
                v = v + rs_in[k, i - 1].astype(F32)
            rs_out[k, i] = v.astype(BF)
            rs_copy(k, i).start()

    def hid_at(k, step):
        return hid.at[:, half_rows(k, core), zcol(step)[1]]

    def ag_copy(k, i):
        if i < ha:
            return remote(hid_at(k, -i), hid_at(k, -i), ag_s.at[k, i], ag_r.at[k, i], fore)
        return remote(hid_at(k, i - ha), hid_at(k, i - ha), ag_s.at[k, i], ag_r.at[k, i], aft)

    def pt_copy(k, step):
        j, _ = zcol(step)
        return remote(hid_at(k, step), hid_at(k, step), pt_s.at[k, j], pt_r.at[k, j], other)

    def arrive(k):
        @pl.loop(max(1, k * per), (k + 1) * per)
        def _(q):
            disp_copy(q).wait_recv()

        fwd_copy(k).start()

    def partials(k):
        fwd_copy(k).wait_recv()
        if k == 0:
            for i in range(3):
                load(i).wait()
                w_copy(i).wait_recv()
        x0, g0, col = split_rows(recv[half_rows(k, core), :], width)
        x1, g1, _ = split_rows(peer[k], width)
        pcol[k] = jnp.broadcast_to(col, (half, LANE))
        part[k, 0] = dot(x0, gw_ref[...]) + dot(x1, pgw[...])
        part[k, 1] = dot(x0, uw_ref[...]) + dot(x1, puw[...])
        part[k, 2] = dot(g0, dw_ref[...], 1, 1) + dot(g1, pdw[...], 1, 1)
        rs_hop(k, 0)

    def swiglu(k):
        rs_copy(k, ha - 1).wait_recv()
        v = part[k, :, :, zcol(0)[1]] + rs_in[k, ha - 1].astype(F32)
        if hb > 0:
            rs_copy(k, ha + hb - 1).wait_recv()
            v = v + rs_in[k, ha + hb - 1].astype(F32)
        gate_pre, up_pre, raw = v[0], v[1], v[2]
        hidden_grad = raw * pcol[k]
        sig = 1.0 / (1.0 + jnp.exp(-gate_pre))
        active = gate_pre * sig * up_pre
        gate_delta = hidden_grad * up_pre * sig * (1.0 + gate_pre * (1.0 - sig))
        up_delta = hidden_grad * gate_pre * sig
        inner = jnp.sum(active * raw, axis=1, keepdims=True)
        shape = (half // BLK, BLK, LANE)
        diag = iota(shape, 1) == iota(shape, 2)
        spread = jnp.broadcast_to(inner, (half, LANE)).reshape(shape)
        line = jnp.sum(jnp.where(diag, spread, 0.0), axis=1, keepdims=True)
        high = line.astype(BF).astype(F32)
        last = iota(shape, 1) == BLK - 1

        def with_line(body, extra):
            return jnp.where(last, extra, body.reshape(shape)).reshape(half, LANE).astype(BF)

        at = (half_rows(k, core), zcol(0)[1])
        hid[(0, *at)] = with_line(active, high)
        hid[(1, *at)] = with_line(gate_delta, line - high)
        hid[(2, *at)] = up_delta.astype(BF)
        ag_copy(k, 0).start()
        if hb > 0:
            ag_copy(k, ha).start()
        pt_copy(k, 0).start()

    def ag_hop(k, h):
        for i, step, hops in ((h, -(h + 1), ha), (ha + h, h + 1, hb)):
            if h >= hops:
                continue
            ag_copy(k, i).wait_recv()
            if h + 1 < hops:
                ag_copy(k, i + 1).start()
            pt_copy(k, step).start()

    def give_back(k):
        for j in range(nz):
            at = hid.at[:, half_rows(k, 1 - core), pl.ds(j * LANE, LANE)]
            remote(at, at, pt_s.at[k, j], pt_r.at[k, j], other).wait_recv()
        mine = pl.ds(k * crows, crows)
        grad = dot(hid[1, mine, :], gw_ref[...], 1, 1) + dot(hid[2, mine, :], uw_ref[...], 1, 1)
        line = hid[0, mine, 0:LANE].astype(F32) + hid[1, mine, 0:LANE].astype(F32)
        for j in range(1, nz):
            at = slice(j * LANE, (j + 1) * LANE)
            line = line + hid[0, mine, at].astype(F32) + hid[1, mine, at].astype(F32)
        wide = jnp.concatenate([line] + [jnp.zeros_like(line)] * (width // LANE - 1), axis=1)
        last = (iota((crows, width), 0) & (BLK - 1)) == BLK - 1
        out = jnp.where(last, wide, grad).astype(BF)
        rgrad[mine, :] = out
        if k == 0:
            back[0:BLK, :] = out[0:BLK]

        @pl.loop(max(1, k * per), (k + 1) * per)
        def _(q):
            ret_copy(q).start()

    stages = [arrive, partials]
    stages += [functools.partial(lambda k, h: rs_hop(k, h), h=h) for h in range(1, ha)]
    stages += [swiglu]
    stages += [functools.partial(lambda k, h: ag_hop(k, h), h=h) for h in range(ha)]
    stages += [give_back]
    for stage, k in PLAN:
        stages[stage](k)

    xs, gs, col = split_rows(recv[...], width)
    scaled = (gs.astype(F32) * col).astype(BF)
    ggrad_ref[...] = dot(xs, hid[1], 0, 0).astype(BF)
    store(0).start()
    ugrad_ref[...] = dot(xs, hid[2], 0, 0).astype(BF)
    store(1).start()
    dgrad_ref[...] = dot(hid[0], scaled, 0, 0).astype(BF)
    store(2).start()

    @pl.loop(1, slots)
    def _(q):
        ret_copy(q).wait_recv()

    picks = sel[slots : slots + toks, :]
    xgrad_ref[...] = dot(picks, back[...]).astype(BF)
    lines = back[...].astype(F32).reshape(slots, BLK, width)[:, BLK - 1, 0:LANE].astype(BF)
    line_x = jnp.where(own_lane, dot(lines, spread, 1, 1), 0.0)
    line_vec = jnp.sum(line_x, axis=0, keepdims=True)
    table = dot((picks.astype(F32) * line_vec).astype(BF), expand, 1, 1)
    result = jnp.zeros((toks, topk), F32)
    k_lane = iota((toks, topk), 1)
    for k in range(topk):
        hit = ids[:, k : k + 1] == named
        value = jnp.sum(jnp.where(hit, table, 0.0), axis=1, keepdims=True)
        result = jnp.where(k_lane == k, value, result)
    pgrad_ref[...] = dot(result.astype(BF), eye, 0, 0).astype(BF)

    for i in range(3):
        store(i).wait()
        w_copy(i).wait_send()

    @pl.loop(1, slots)
    def _(q):
        disp_copy(q).wait_send()
        ret_copy(q).wait_send()

    for k in range(chunks):
        fwd_copy(k).wait_send()
        for i in range(ha + hb):
            rs_copy(k, i).wait_send()
            ag_copy(k, i).wait_send()
        for j in range(nz):
            at = hid.at[:, half_rows(k, core), pl.ds(j * LANE, LANE)]
            remote(at, at, pt_s.at[k, j], pt_r.at[k, j], other).wait_send()


def copy_out(*refs):
    n = (len(refs) - 2) // 3
    srcs, dsts, held = refs[:n], refs[n : 2 * n], refs[2 * n : 3 * n]
    ins = [pltpu.make_async_copy(srcs[i], held[i], refs[3 * n].at[i]) for i in range(n)]
    outs = [pltpu.make_async_copy(held[i], dsts[i], refs[3 * n + 1].at[i]) for i in range(n)]
    for i in range(n):
        ins[i].start()
    for i in range(n):
        ins[i].wait()
        outs[i].start()
    for i in range(n):
        outs[i].wait()


def on_device(sizes, layer_input, output_grad, route_ids, route_probs, gate_weight, up_weight, down_weight):
    nx, ny, nz = sizes
    toks, width = layer_input.shape
    hidden = gate_weight.shape[2]
    topk = route_ids.shape[1]
    slots = nx * ny
    rows = slots * BLK
    chunks = ny // 2
    half = nx * BLK
    hops = nz - 1
    assert hidden == nz * LANE
    assert 3 * toks * topk // (2 * slots) < BLK
    assert (chunks, nz) == (4, 8)
    vmem = pl.BlockSpec(memory_space=pltpu.VMEM)
    anyw = pl.BlockSpec(memory_space=pl.ANY)
    dma = pltpu.SemaphoreType.DMA
    out_shape = (
        jax.ShapeDtypeStruct((toks, width), BF),
        jax.ShapeDtypeStruct((topk, toks), BF),
        jax.ShapeDtypeStruct((width, hidden), BF),
        jax.ShapeDtypeStruct((width, hidden), BF),
        jax.ShapeDtypeStruct((hidden, width), BF),
    )
    outs = pl.pallas_call(
        functools.partial(kernel, nx, ny, nz),
        out_shape=out_shape,
        in_specs=[vmem] * 4 + [anyw] * 3,
        out_specs=[vmem] * 2 + [anyw] * 3,
        scratch_shapes=[
            pltpu.VMEM((slots + toks, 2 * width), BF),
            pltpu.VMEM((slots + toks, rows), BF),
            pltpu.VMEM((rows, 2 * width), BF),
            pltpu.VMEM((rows, 2 * width), BF),
            pltpu.VMEM((chunks, half, 2 * width), BF),
            pltpu.VMEM((chunks, 3, half, hidden), F32),
            pltpu.VMEM((chunks, hops, 3, half, LANE), BF),
            pltpu.VMEM((chunks, hops, 3, half, LANE), BF),
            pltpu.VMEM((3, rows, hidden), BF),
            pltpu.VMEM((rows, width), BF),
            pltpu.VMEM((rows, width), BF),
            pltpu.VMEM((width, hidden), BF),
            pltpu.VMEM((width, hidden), BF),
            pltpu.VMEM((hidden, width), BF),
            pltpu.VMEM((chunks, half, LANE), F32),
            pltpu.VMEM((width, hidden), BF),
            pltpu.VMEM((width, hidden), BF),
            pltpu.VMEM((hidden, width), BF),
            pltpu.VMEM((width, hidden), BF),
            pltpu.VMEM((width, hidden), BF),
            pltpu.VMEM((hidden, width), BF),
            dma((3,)), dma((3,)),
            dma((slots,)), dma((slots,)), dma((slots,)), dma((slots,)),
            dma((3,)), dma((3,)),
            dma((chunks,)), dma((chunks,)),
            dma((chunks, hops)), dma((chunks, hops)),
            dma((chunks, hops)), dma((chunks, hops)),
            dma((chunks, nz)), dma((chunks, nz)),
        ],
        compiler_params=pltpu.CompilerParams(
            collective_id=0, has_side_effects=True, vmem_limit_bytes=60 * 1024 * 1024
        ),
    )(
        layer_input, output_grad, route_ids.T, route_probs.T,
        gate_weight[0], up_weight[0], down_weight[0],
    )
    xgrad, pgrad, ggrad, ugrad, dgrad = pl.pallas_call(
        copy_out,
        out_shape=out_shape,
        in_specs=[anyw] * 5,
        out_specs=[anyw] * 5,
        scratch_shapes=[pltpu.VMEM(o.shape, o.dtype) for o in out_shape] + [dma((5,)), dma((5,))],
    )(*outs)
    return (xgrad, pgrad.T, ggrad[None], ugrad[None], dgrad[None])


def solution(mesh, sizes=(4, 8, 8)):
    placed = (
        P("expert", "dp"),
        P("expert", "dp"),
        P("expert", None),
        P("expert", None),
        P("expert", "dp", None),
        P("expert", "dp", None),
        P("expert", None, "dp"),
    )
    return jax.shard_map(
        functools.partial(on_device, sizes),
        mesh=mesh,
        in_specs=placed,
        out_specs=(
            P("expert", "dp"),
            P("expert", None),
            P("expert", "dp", None),
            P("expert", "dp", None),
            P("expert", None, "dp"),
        ),
        check_vma=False,
    )
```

```python
import functools

import jax
import jax.numpy as jnp
from jax import lax
from jax.experimental import pallas as pl
from jax.experimental.pallas import tpu as pltpu
from jax.sharding import PartitionSpec as P

MESH = pl.DeviceIdType.MESH
BF = jnp.bfloat16
F32 = jnp.float32
BLK = 16
LANE = 128


def log2(n):
    return n.bit_length() - 1


def dot(a, b, ca=1, cb=0):
    return lax.dot_general(a, b, (((ca,), (cb,)), ((), ())), preferred_element_type=F32)


def iota(shape, dim):
    return lax.broadcasted_iota(jnp.int32, shape, dim)


def split_rows(block, width):
    rows = block.shape[0]
    x = block[:, :width].astype(F32)
    g = block[:, width:]
    head = x[:, :LANE].reshape(rows // BLK, BLK, LANE)
    shape = head.shape
    diag = iota(shape, 1) == iota(shape, 2)
    spread = jnp.broadcast_to(head[:, BLK - 1 :, :], shape)
    col = jnp.sum(jnp.where(diag, spread, 0.0), axis=2, keepdims=True).reshape(rows, 1)
    keep = (iota(x.shape, 0) & (BLK - 1)) != BLK - 1
    return jnp.where(keep, x, 0.0).astype(BF), g, col


def kernel(
    nx, ny, nz,
    x_ref, g_ref, ids_ref, prob_ref, gate_hbm, up_hbm, down_hbm,
    xgrad_ref, pgrad_ref, ggrad_hbm, ugrad_hbm, dgrad_hbm,
    tok, sel, send, recv, peer, part, rs_in, rs_out, hid, rgrad, back, pgw, puw, pdw, pcol,
    gw_ref, uw_ref, dw_ref, ggrad_ref, ugrad_ref, dgrad_ref, in_s, out_s,
    disp_s, disp_r, ret_s, ret_r, w_s, w_r, fwd_s, fwd_r, rs_s, rs_r, ag_s, ag_r, pt_s, pt_r,
):
    toks, width = x_ref.shape
    topk = ids_ref.shape[0]
    slots = nx * ny
    rows = slots * BLK
    chunks = ny // 2
    half = nx * BLK
    crows = 2 * half
    per = 2 * nx
    ha, hb = nz // 2, nz // 2 - 1
    lx = log2(nx)

    dp = lax.axis_index("dp")
    ex = lax.axis_index("expert")
    z, core = dp // 2, dp % 2
    mx, my = ex // ny, ex % ny
    s = 1 - 2 * core

    def zdev(step):
        return {"dp": ((z + step * s + nz) % nz) * 2 + core}

    fore, aft = zdev(1), zdev(-1)
    other = {"dp": z * 2 + 1 - core}

    def offset(q):
        c, b, dx = q // per, (q // nx) % 2, q % nx
        dy = jnp.where(b == 0, -c, c + 1)
        return dx, dy

    def target(q):
        dx, dy = offset(q)
        return {"expert": ((mx + dx) % nx) * ny + (my + dy + ny) % ny}

    def origin(q):
        dx, dy = offset(q)
        return {"expert": ((mx - dx + nx) % nx) * ny + (my - dy + ny) % ny}

    def remote(src, dst, ssem, rsem, dev):
        return pltpu.make_async_remote_copy(
            src_ref=src, dst_ref=dst, send_sem=ssem, recv_sem=rsem, device_id=dev, device_id_type=MESH
        )

    loads = ((gate_hbm, gw_ref), (up_hbm, uw_ref), (down_hbm, dw_ref))
    stores = ((ggrad_ref, ggrad_hbm), (ugrad_ref, ugrad_hbm), (dgrad_ref, dgrad_hbm))

    def load(i):
        return pltpu.make_async_copy(*loads[i], in_s.at[i])

    def store(i):
        return pltpu.make_async_copy(*stores[i], out_s.at[i])

    barrier = pltpu.get_barrier_semaphore()

    @pl.loop(1, slots)
    def _(q):
        pl.semaphore_signal(barrier, inc=1, device_id=target(q), device_id_type=MESH)

    for dev in (fore, aft, other):
        pl.semaphore_signal(barrier, inc=1, device_id=dev, device_id_type=MESH)

    for i in range(3):
        load(i).start()

    q_lane = iota((toks, slots), 1)
    c_l, b_l, dx_l = q_lane >> (lx + 1), (q_lane >> lx) & 1, q_lane & (nx - 1)
    dy_l = jnp.where(b_l == 0, -c_l, c_l + 1)
    named = (((mx + dx_l) & (nx - 1)) * ny + ((my + dy_l) & (ny - 1))).astype(F32)
    eye = jnp.where(iota((toks, toks), 0) == iota((toks, toks), 1), 1.0, 0.0).astype(BF)
    ids = dot(eye, ids_ref[...].astype(F32).astype(BF), 1, 1)
    prob = dot(eye, prob_ref[...], 1, 1)
    member = jnp.zeros((toks, slots), F32)
    weight = jnp.zeros((toks, slots), F32)
    for k in range(topk):
        hit = ids[:, k : k + 1] == named
        member = member + jnp.where(hit, 1.0, 0.0)
        weight = weight + jnp.where(hit, prob[:, k : k + 1], 0.0)
    lower = jnp.where(iota((toks, toks), 1) < iota((toks, toks), 0), 1.0, 0.0).astype(BF)
    before = dot(lower, member.astype(BF))
    slot = jnp.where(member > 0.0, before, -1.0)
    own_lane = (iota((slots, rows), 1) >> 4) == iota((slots, rows), 0)
    expand = jnp.where(own_lane, 1.0, 0.0).astype(BF)
    slot_x = dot(slot.astype(BF), expand)
    lane16 = (iota((toks, rows), 1) & (BLK - 1)).astype(F32)
    chosen = slot_x == lane16
    weight_x = dot(weight.astype(BF), expand)
    prob_vec = jnp.sum(jnp.where(chosen, weight_x, 0.0), axis=0, keepdims=True)
    spread = jnp.where((iota((rows, LANE), 0) & (BLK - 1)) == iota((rows, LANE), 1), 1.0, 0.0).astype(BF)
    prob_rows = dot(jnp.where(own_lane, prob_vec, 0.0).astype(BF), spread)
    scalar_lane = iota((slots, rows), 1) == iota((slots, rows), 0) * BLK + (BLK - 1)
    sel[0:slots, :] = jnp.where(scalar_lane, 1.0, 0.0).astype(BF)
    sel[slots : slots + toks, :] = jnp.where(chosen, 1.0, 0.0).astype(BF)
    tok[0:slots, :] = jnp.zeros((slots, 2 * width), BF)
    tok[0:slots, 0:LANE] = prob_rows.astype(BF)
    tok[slots : slots + toks, 0:width] = x_ref[...]
    tok[slots : slots + toks, width : 2 * width] = g_ref[...]
    packed = dot(sel[...], tok[...], 0, 0).astype(BF)
    send[...] = packed
    recv[0:BLK, :] = packed[0:BLK]

    pl.semaphore_wait(barrier, slots - 1 + 3)

    def w_copy(i):
        src, dst = ((gw_ref, pgw), (uw_ref, puw), (dw_ref, pdw))[i]
        return remote(src, dst, w_s.at[i], w_r.at[i], other)

    def block(q):
        return pl.ds(pl.multiple_of(q * BLK, BLK), BLK)

    def disp_copy(q):
        return remote(send.at[block(q)], recv.at[block(q)], disp_s.at[q], disp_r.at[q], target(q))

    def ret_copy(q):
        return remote(rgrad.at[block(q)], back.at[block(q)], ret_s.at[q], ret_r.at[q], origin(q))

    for i in range(3):
        load(i).wait()
        w_copy(i).start()

    @pl.loop(1, slots)
    def _(q):
        disp_copy(q).start()

    def half_rows(k, h):
        return pl.ds(pl.multiple_of(k * crows + h * half, BLK), half)

    def fwd_copy(k):
        return remote(recv.at[half_rows(k, 1 - core)], peer.at[k], fwd_s.at[k], fwd_r.at[k], other)

    def zcol(step):
        j = (z + step * s + nz) % nz
        return j, pl.ds(pl.multiple_of(j * LANE, LANE), LANE)

    def rs_copy(k, i):
        return remote(rs_out.at[k, i], rs_in.at[k, i], rs_s.at[k, i], rs_r.at[k, i], fore if i < ha else aft)

    def rs_hop(k, h):
        for i, step, hops in ((h, ha - h, ha), (ha + h, h - hb, hb)):
            if h >= hops:
                continue
            v = part[k, :, :, zcol(step)[1]]
            if h > 0:
                rs_copy(k, i - 1).wait_recv()
                v = v + rs_in[k, i - 1].astype(F32)
            rs_out[k, i] = v.astype(BF)
            rs_copy(k, i).start()

    def hid_at(k, step):
        return hid.at[:, half_rows(k, core), zcol(step)[1]]

    def ag_copy(k, i):
        if i < ha:
            return remote(hid_at(k, -i), hid_at(k, -i), ag_s.at[k, i], ag_r.at[k, i], fore)
        return remote(hid_at(k, i - ha), hid_at(k, i - ha), ag_s.at[k, i], ag_r.at[k, i], aft)

    def pt_copy(k, step):
        j, _ = zcol(step)
        return remote(hid_at(k, step), hid_at(k, step), pt_s.at[k, j], pt_r.at[k, j], other)

    def arrive(k):
        @pl.loop(max(1, k * per), (k + 1) * per)
        def _(q):
            disp_copy(q).wait_recv()

        fwd_copy(k).start()

    def partials(k):
        fwd_copy(k).wait_recv()
        if k == 0:
            for i in range(3):
                w_copy(i).wait_recv()
        x0, g0, col = split_rows(recv[half_rows(k, core), :], width)
        x1, g1, _ = split_rows(peer[k], width)
        pcol[k] = jnp.broadcast_to(col, (half, LANE))
        part[k, 0] = dot(x0, gw_ref[...]) + dot(x1, pgw[...])
        part[k, 1] = dot(x0, uw_ref[...]) + dot(x1, puw[...])
        part[k, 2] = dot(g0, dw_ref[...], 1, 1) + dot(g1, pdw[...], 1, 1)
        rs_hop(k, 0)

    def swiglu(k):
        rs_copy(k, ha - 1).wait_recv()
        v = part[k, :, :, zcol(0)[1]] + rs_in[k, ha - 1].astype(F32)
        if hb > 0:
            rs_copy(k, ha + hb - 1).wait_recv()
            v = v + rs_in[k, ha + hb - 1].astype(F32)
        gate_pre, up_pre, raw = v[0], v[1], v[2]
        hidden_grad = raw * pcol[k]
        sig = 1.0 / (1.0 + jnp.exp(-gate_pre))
        active = gate_pre * sig * up_pre
        gate_delta = hidden_grad * up_pre * sig * (1.0 + gate_pre * (1.0 - sig))
        up_delta = hidden_grad * gate_pre * sig
        inner = jnp.sum(active * raw, axis=1, keepdims=True)
        shape = (half // BLK, BLK, LANE)
        diag = iota(shape, 1) == iota(shape, 2)
        spread = jnp.broadcast_to(inner, (half, LANE)).reshape(shape)
        line = jnp.sum(jnp.where(diag, spread, 0.0), axis=1, keepdims=True)
        high = line.astype(BF).astype(F32)
        last = iota(shape, 1) == BLK - 1

        def with_line(body, extra):
            return jnp.where(last, extra, body.reshape(shape)).reshape(half, LANE).astype(BF)

        at = (half_rows(k, core), zcol(0)[1])
        hid[(0, *at)] = with_line(active, high)
        hid[(1, *at)] = with_line(gate_delta, line - high)
        hid[(2, *at)] = up_delta.astype(BF)
        ag_copy(k, 0).start()
        if hb > 0:
            ag_copy(k, ha).start()
        pt_copy(k, 0).start()

    def ag_hop(k, h):
        for i, step, hops in ((h, -(h + 1), ha), (ha + h, h + 1, hb)):
            if h >= hops:
                continue
            ag_copy(k, i).wait_recv()
            if h + 1 < hops:
                ag_copy(k, i + 1).start()
            pt_copy(k, step).start()

    def give_back(k):
        for j in range(nz):
            at = hid.at[:, half_rows(k, 1 - core), pl.ds(j * LANE, LANE)]
            remote(at, at, pt_s.at[k, j], pt_r.at[k, j], other).wait_recv()
        mine = pl.ds(k * crows, crows)
        grad = dot(hid[1, mine, :], gw_ref[...], 1, 1) + dot(hid[2, mine, :], uw_ref[...], 1, 1)
        line = hid[0, mine, 0:LANE].astype(F32) + hid[1, mine, 0:LANE].astype(F32)
        for j in range(1, nz):
            at = slice(j * LANE, (j + 1) * LANE)
            line = line + hid[0, mine, at].astype(F32) + hid[1, mine, at].astype(F32)
        wide = jnp.concatenate([line] + [jnp.zeros_like(line)] * (width // LANE - 1), axis=1)
        last = (iota((crows, width), 0) & (BLK - 1)) == BLK - 1
        out = jnp.where(last, wide, grad).astype(BF)
        rgrad[mine, :] = out
        if k == 0:
            back[0:BLK, :] = out[0:BLK]

        @pl.loop(max(1, k * per), (k + 1) * per)
        def _(q):
            ret_copy(q).start()

    stages = [arrive, partials]
    stages += [functools.partial(lambda k, h: rs_hop(k, h), h=h) for h in range(1, ha)]
    stages += [swiglu]
    stages += [functools.partial(lambda k, h: ag_hop(k, h), h=h) for h in range(ha)]
    stages += [give_back]
    for tick in range(len(stages) + chunks - 1):
        for k in range(chunks):
            if 0 <= tick - k < len(stages):
                stages[tick - k](k)

    xs, gs, col = split_rows(recv[...], width)
    scaled = (gs.astype(F32) * col).astype(BF)
    ggrad_ref[...] = dot(xs, hid[1], 0, 0).astype(BF)
    store(0).start()
    ugrad_ref[...] = dot(xs, hid[2], 0, 0).astype(BF)
    store(1).start()
    dgrad_ref[...] = dot(hid[0], scaled, 0, 0).astype(BF)
    store(2).start()

    @pl.loop(1, slots)
    def _(q):
        ret_copy(q).wait_recv()

    picks = sel[slots : slots + toks, :]
    xgrad_ref[...] = dot(picks, back[...]).astype(BF)
    lines = back[...].astype(F32).reshape(slots, BLK, width)[:, BLK - 1, 0:LANE].astype(BF)
    line_x = jnp.where(own_lane, dot(lines, spread, 1, 1), 0.0)
    line_vec = jnp.sum(line_x, axis=0, keepdims=True)
    table = dot((picks.astype(F32) * line_vec).astype(BF), expand, 1, 1)
    result = jnp.zeros((toks, topk), F32)
    k_lane = iota((toks, topk), 1)
    for k in range(topk):
        hit = ids[:, k : k + 1] == named
        value = jnp.sum(jnp.where(hit, table, 0.0), axis=1, keepdims=True)
        result = jnp.where(k_lane == k, value, result)
    pgrad_ref[...] = dot(result.astype(BF), eye, 0, 0).astype(BF)

    for i in range(3):
        store(i).wait()
        w_copy(i).wait_send()

    @pl.loop(1, slots)
    def _(q):
        disp_copy(q).wait_send()
        ret_copy(q).wait_send()

    for k in range(chunks):
        fwd_copy(k).wait_send()
        for i in range(ha + hb):
            rs_copy(k, i).wait_send()
            ag_copy(k, i).wait_send()
        for j in range(nz):
            at = hid.at[:, half_rows(k, core), pl.ds(j * LANE, LANE)]
            remote(at, at, pt_s.at[k, j], pt_r.at[k, j], other).wait_send()


def copy_out(*refs):
    n = (len(refs) - 2) // 3
    srcs, dsts, held = refs[:n], refs[n : 2 * n], refs[2 * n : 3 * n]
    ins = [pltpu.make_async_copy(srcs[i], held[i], refs[3 * n].at[i]) for i in range(n)]
    outs = [pltpu.make_async_copy(held[i], dsts[i], refs[3 * n + 1].at[i]) for i in range(n)]
    for i in range(n):
        ins[i].start()
    for i in range(n):
        ins[i].wait()
        outs[i].start()
    for i in range(n):
        outs[i].wait()


def on_device(sizes, layer_input, output_grad, route_ids, route_probs, gate_weight, up_weight, down_weight):
    nx, ny, nz = sizes
    toks, width = layer_input.shape
    hidden = gate_weight.shape[2]
    topk = route_ids.shape[1]
    slots = nx * ny
    rows = slots * BLK
    chunks = ny // 2
    half = nx * BLK
    hops = nz - 1
    assert hidden == nz * LANE
    assert 3 * toks * topk // (2 * slots) < BLK
    vmem = pl.BlockSpec(memory_space=pltpu.VMEM)
    anyw = pl.BlockSpec(memory_space=pl.ANY)
    dma = pltpu.SemaphoreType.DMA
    out_shape = (
        jax.ShapeDtypeStruct((toks, width), BF),
        jax.ShapeDtypeStruct((topk, toks), BF),
        jax.ShapeDtypeStruct((width, hidden), BF),
        jax.ShapeDtypeStruct((width, hidden), BF),
        jax.ShapeDtypeStruct((hidden, width), BF),
    )
    outs = pl.pallas_call(
        functools.partial(kernel, nx, ny, nz),
        out_shape=out_shape,
        in_specs=[vmem] * 4 + [anyw] * 3,
        out_specs=[vmem] * 2 + [anyw] * 3,
        scratch_shapes=[
            pltpu.VMEM((slots + toks, 2 * width), BF),
            pltpu.VMEM((slots + toks, rows), BF),
            pltpu.VMEM((rows, 2 * width), BF),
            pltpu.VMEM((rows, 2 * width), BF),
            pltpu.VMEM((chunks, half, 2 * width), BF),
            pltpu.VMEM((chunks, 3, half, hidden), F32),
            pltpu.VMEM((chunks, hops, 3, half, LANE), BF),
            pltpu.VMEM((chunks, hops, 3, half, LANE), BF),
            pltpu.VMEM((3, rows, hidden), BF),
            pltpu.VMEM((rows, width), BF),
            pltpu.VMEM((rows, width), BF),
            pltpu.VMEM((width, hidden), BF),
            pltpu.VMEM((width, hidden), BF),
            pltpu.VMEM((hidden, width), BF),
            pltpu.VMEM((chunks, half, LANE), F32),
            pltpu.VMEM((width, hidden), BF),
            pltpu.VMEM((width, hidden), BF),
            pltpu.VMEM((hidden, width), BF),
            pltpu.VMEM((width, hidden), BF),
            pltpu.VMEM((width, hidden), BF),
            pltpu.VMEM((hidden, width), BF),
            dma((3,)), dma((3,)),
            dma((slots,)), dma((slots,)), dma((slots,)), dma((slots,)),
            dma((3,)), dma((3,)),
            dma((chunks,)), dma((chunks,)),
            dma((chunks, hops)), dma((chunks, hops)),
            dma((chunks, hops)), dma((chunks, hops)),
            dma((chunks, nz)), dma((chunks, nz)),
        ],
        compiler_params=pltpu.CompilerParams(
            collective_id=0, has_side_effects=True, vmem_limit_bytes=60 * 1024 * 1024
        ),
    )(
        layer_input, output_grad, route_ids.T, route_probs.T,
        gate_weight[0], up_weight[0], down_weight[0],
    )
    xgrad, pgrad, ggrad, ugrad, dgrad = pl.pallas_call(
        copy_out,
        out_shape=out_shape,
        in_specs=[anyw] * 5,
        out_specs=[anyw] * 5,
        scratch_shapes=[pltpu.VMEM(o.shape, o.dtype) for o in out_shape] + [dma((5,)), dma((5,))],
    )(*outs)
    return (xgrad, pgrad.T, ggrad[None], ugrad[None], dgrad[None])


def solution(mesh, sizes=(4, 8, 8)):
    placed = (
        P("expert", "dp"),
        P("expert", "dp"),
        P("expert", None),
        P("expert", None),
        P("expert", "dp", None),
        P("expert", "dp", None),
        P("expert", None, "dp"),
    )
    return jax.shard_map(
        functools.partial(on_device, sizes),
        mesh=mesh,
        in_specs=placed,
        out_specs=(
            P("expert", "dp"),
            P("expert", None),
            P("expert", "dp", None),
            P("expert", "dp", None),
            P("expert", None, "dp"),
        ),
        check_vma=False,
    )
```

```python
import functools

import jax
import jax.numpy as jnp
from jax import lax
from jax.experimental import pallas as pl
from jax.experimental.pallas import tpu as pltpu
from jax.sharding import PartitionSpec as P

MESH = pl.DeviceIdType.MESH
BF = jnp.bfloat16
F32 = jnp.float32
BLK = 16
LANE = 128


def log2(n):
    return n.bit_length() - 1


def dot(a, b, ca=1, cb=0):
    return lax.dot_general(a, b, (((ca,), (cb,)), ((), ())), preferred_element_type=F32)


def iota(shape, dim):
    return lax.broadcasted_iota(jnp.int32, shape, dim)


def split_rows(block, width):
    rows = block.shape[0]
    x = block[:, :width].astype(F32)
    g = block[:, width:]
    head = x[:, :LANE].reshape(rows // BLK, BLK, LANE)
    shape = head.shape
    diag = iota(shape, 1) == iota(shape, 2)
    spread = jnp.broadcast_to(head[:, BLK - 1 :, :], shape)
    col = jnp.sum(jnp.where(diag, spread, 0.0), axis=2, keepdims=True).reshape(rows, 1)
    keep = (iota(x.shape, 0) & (BLK - 1)) != BLK - 1
    return jnp.where(keep, x, 0.0).astype(BF), g, col


def kernel(
    nx, ny, nz,
    x_ref, g_ref, ids_ref, prob_ref, gate_hbm, up_hbm, down_hbm,
    xgrad_ref, pgrad_ref, ggrad_hbm, ugrad_hbm, dgrad_hbm,
    tok, sel, send, recv, peer, part, rs_in, rs_out, hid, rgrad, back, pgw, puw, pdw, pcol,
    gw_ref, uw_ref, dw_ref, ggrad_ref, ugrad_ref, dgrad_ref, in_s, out_s,
    disp_s, disp_r, ret_s, ret_r, w_s, w_r, fwd_s, fwd_r, rs_s, rs_r, ag_s, ag_r, pt_s, pt_r,
):
    toks, width = x_ref.shape
    topk = ids_ref.shape[0]
    slots = nx * ny
    rows = slots * BLK
    chunks = ny // 2
    half = nx * BLK
    crows = 2 * half
    per = 2 * nx
    ha, hb = nz // 2, nz // 2 - 1
    lx = log2(nx)

    dp = lax.axis_index("dp")
    ex = lax.axis_index("expert")
    z, core = dp // 2, dp % 2
    mx, my = ex // ny, ex % ny
    s = 1 - 2 * core

    def zdev(step):
        return {"dp": ((z + step * s + nz) % nz) * 2 + core}

    fore, aft = zdev(1), zdev(-1)
    other = {"dp": z * 2 + 1 - core}

    def reach(c):
        return jnp.where(c == chunks - 1, 1, jnp.where(c == 0, 0, c + 1))

    def offset(q):
        c, b, dx = q // per, (q // nx) % 2, q % nx
        far = reach(c)
        dy = jnp.where(b == 0, -far, far + 1)
        return dx, dy

    def target(q):
        dx, dy = offset(q)
        return {"expert": ((mx + dx) % nx) * ny + (my + dy + ny) % ny}

    def origin(q):
        dx, dy = offset(q)
        return {"expert": ((mx - dx + nx) % nx) * ny + (my - dy + ny) % ny}

    def remote(src, dst, ssem, rsem, dev):
        return pltpu.make_async_remote_copy(
            src_ref=src, dst_ref=dst, send_sem=ssem, recv_sem=rsem, device_id=dev, device_id_type=MESH
        )

    loads = ((gate_hbm, gw_ref), (up_hbm, uw_ref), (down_hbm, dw_ref))
    stores = ((ggrad_ref, ggrad_hbm), (ugrad_ref, ugrad_hbm), (dgrad_ref, dgrad_hbm))

    def load(i):
        return pltpu.make_async_copy(*loads[i], in_s.at[i])

    def store(i):
        return pltpu.make_async_copy(*stores[i], out_s.at[i])

    barrier = pltpu.get_barrier_semaphore()

    @pl.loop(1, slots)
    def _(q):
        pl.semaphore_signal(barrier, inc=1, device_id=target(q), device_id_type=MESH)

    for dev in (fore, aft, other):
        pl.semaphore_signal(barrier, inc=1, device_id=dev, device_id_type=MESH)

    for i in range(3):
        load(i).start()

    q_lane = iota((toks, slots), 1)
    c_l, b_l, dx_l = q_lane >> (lx + 1), (q_lane >> lx) & 1, q_lane & (nx - 1)
    dy_l = jnp.where(b_l == 0, -reach(c_l), reach(c_l) + 1)
    named = (((mx + dx_l) & (nx - 1)) * ny + ((my + dy_l) & (ny - 1))).astype(F32)
    eye = jnp.where(iota((toks, toks), 0) == iota((toks, toks), 1), 1.0, 0.0).astype(BF)
    ids = dot(eye, ids_ref[...].astype(F32).astype(BF), 1, 1)
    prob = dot(eye, prob_ref[...], 1, 1)
    member = jnp.zeros((toks, slots), F32)
    weight = jnp.zeros((toks, slots), F32)
    for k in range(topk):
        hit = ids[:, k : k + 1] == named
        member = member + jnp.where(hit, 1.0, 0.0)
        weight = weight + jnp.where(hit, prob[:, k : k + 1], 0.0)
    lower = jnp.where(iota((toks, toks), 1) < iota((toks, toks), 0), 1.0, 0.0).astype(BF)
    before = dot(lower, member.astype(BF))
    slot = jnp.where(member > 0.0, before, -1.0)
    own_lane = (iota((slots, rows), 1) >> 4) == iota((slots, rows), 0)
    expand = jnp.where(own_lane, 1.0, 0.0).astype(BF)
    slot_x = dot(slot.astype(BF), expand)
    lane16 = (iota((toks, rows), 1) & (BLK - 1)).astype(F32)
    chosen = slot_x == lane16
    weight_x = dot(weight.astype(BF), expand)
    prob_vec = jnp.sum(jnp.where(chosen, weight_x, 0.0), axis=0, keepdims=True)
    spread = jnp.where((iota((rows, LANE), 0) & (BLK - 1)) == iota((rows, LANE), 1), 1.0, 0.0).astype(BF)
    prob_rows = dot(jnp.where(own_lane, prob_vec, 0.0).astype(BF), spread)
    scalar_lane = iota((slots, rows), 1) == iota((slots, rows), 0) * BLK + (BLK - 1)
    sel[0:slots, :] = jnp.where(scalar_lane, 1.0, 0.0).astype(BF)
    sel[slots : slots + toks, :] = jnp.where(chosen, 1.0, 0.0).astype(BF)
    tok[0:slots, :] = jnp.zeros((slots, 2 * width), BF)
    tok[0:slots, 0:LANE] = prob_rows.astype(BF)
    tok[slots : slots + toks, 0:width] = x_ref[...]
    tok[slots : slots + toks, width : 2 * width] = g_ref[...]
    packed = dot(sel[...], tok[...], 0, 0).astype(BF)
    send[...] = packed
    recv[0:BLK, :] = packed[0:BLK]

    pl.semaphore_wait(barrier, slots - 1 + 3)

    def w_copy(i):
        src, dst = ((gw_ref, pgw), (uw_ref, puw), (dw_ref, pdw))[i]
        return remote(src, dst, w_s.at[i], w_r.at[i], other)

    def block(q):
        return pl.ds(pl.multiple_of(q * BLK, BLK), BLK)

    def disp_copy(q):
        return remote(send.at[block(q)], recv.at[block(q)], disp_s.at[q], disp_r.at[q], target(q))

    def ret_copy(q):
        return remote(rgrad.at[block(q)], back.at[block(q)], ret_s.at[q], ret_r.at[q], origin(q))

    for i in range(3):
        load(i).wait()
        w_copy(i).start()

    @pl.loop(1, slots)
    def _(q):
        disp_copy(q).start()

    def half_rows(k, h):
        return pl.ds(pl.multiple_of(k * crows + h * half, BLK), half)

    def fwd_copy(k):
        return remote(recv.at[half_rows(k, 1 - core)], peer.at[k], fwd_s.at[k], fwd_r.at[k], other)

    def zcol(step):
        j = (z + step * s + nz) % nz
        return j, pl.ds(pl.multiple_of(j * LANE, LANE), LANE)

    def rs_copy(k, i):
        return remote(rs_out.at[k, i], rs_in.at[k, i], rs_s.at[k, i], rs_r.at[k, i], fore if i < ha else aft)

    def rs_hop(k, h):
        for i, step, hops in ((h, ha - h, ha), (ha + h, h - hb, hb)):
            if h >= hops:
                continue
            v = part[k, :, :, zcol(step)[1]]
            if h > 0:
                rs_copy(k, i - 1).wait_recv()
                v = v + rs_in[k, i - 1].astype(F32)
            rs_out[k, i] = v.astype(BF)
            rs_copy(k, i).start()

    def hid_at(k, step):
        return hid.at[:, half_rows(k, core), zcol(step)[1]]

    def ag_copy(k, i):
        if i < ha:
            return remote(hid_at(k, -i), hid_at(k, -i), ag_s.at[k, i], ag_r.at[k, i], fore)
        return remote(hid_at(k, i - ha), hid_at(k, i - ha), ag_s.at[k, i], ag_r.at[k, i], aft)

    def pt_copy(k, step):
        j, _ = zcol(step)
        return remote(hid_at(k, step), hid_at(k, step), pt_s.at[k, j], pt_r.at[k, j], other)

    def arrive(k):
        @pl.loop(max(1, k * per), (k + 1) * per)
        def _(q):
            disp_copy(q).wait_recv()

        fwd_copy(k).start()

    def partials(k):
        fwd_copy(k).wait_recv()
        if k == 0:
            for i in range(3):
                w_copy(i).wait_recv()
        x0, g0, col = split_rows(recv[half_rows(k, core), :], width)
        x1, g1, _ = split_rows(peer[k], width)
        pcol[k] = jnp.broadcast_to(col, (half, LANE))
        part[k, 0] = dot(x0, gw_ref[...]) + dot(x1, pgw[...])
        part[k, 1] = dot(x0, uw_ref[...]) + dot(x1, puw[...])
        part[k, 2] = dot(g0, dw_ref[...], 1, 1) + dot(g1, pdw[...], 1, 1)
        rs_hop(k, 0)

    def swiglu(k):
        rs_copy(k, ha - 1).wait_recv()
        v = part[k, :, :, zcol(0)[1]] + rs_in[k, ha - 1].astype(F32)
        if hb > 0:
            rs_copy(k, ha + hb - 1).wait_recv()
            v = v + rs_in[k, ha + hb - 1].astype(F32)
        gate_pre, up_pre, raw = v[0], v[1], v[2]
        hidden_grad = raw * pcol[k]
        sig = 1.0 / (1.0 + jnp.exp(-gate_pre))
        active = gate_pre * sig * up_pre
        gate_delta = hidden_grad * up_pre * sig * (1.0 + gate_pre * (1.0 - sig))
        up_delta = hidden_grad * gate_pre * sig
        inner = jnp.sum(active * raw, axis=1, keepdims=True)
        shape = (half // BLK, BLK, LANE)
        diag = iota(shape, 1) == iota(shape, 2)
        spread = jnp.broadcast_to(inner, (half, LANE)).reshape(shape)
        line = jnp.sum(jnp.where(diag, spread, 0.0), axis=1, keepdims=True)
        high = line.astype(BF).astype(F32)
        last = iota(shape, 1) == BLK - 1

        def with_line(body, extra):
            return jnp.where(last, extra, body.reshape(shape)).reshape(half, LANE).astype(BF)

        at = (half_rows(k, core), zcol(0)[1])
        hid[(0, *at)] = with_line(active, high)
        hid[(1, *at)] = with_line(gate_delta, line - high)
        hid[(2, *at)] = up_delta.astype(BF)
        ag_copy(k, 0).start()
        if hb > 0:
            ag_copy(k, ha).start()
        pt_copy(k, 0).start()

    def ag_hop(k, h):
        for i, step, hops in ((h, -(h + 1), ha), (ha + h, h + 1, hb)):
            if h >= hops:
                continue
            ag_copy(k, i).wait_recv()
            if h + 1 < hops:
                ag_copy(k, i + 1).start()
            pt_copy(k, step).start()

    def give_back(k):
        for j in range(nz):
            at = hid.at[:, half_rows(k, 1 - core), pl.ds(j * LANE, LANE)]
            remote(at, at, pt_s.at[k, j], pt_r.at[k, j], other).wait_recv()
        mine = pl.ds(k * crows, crows)
        grad = dot(hid[1, mine, :], gw_ref[...], 1, 1) + dot(hid[2, mine, :], uw_ref[...], 1, 1)
        line = hid[0, mine, 0:LANE].astype(F32) + hid[1, mine, 0:LANE].astype(F32)
        for j in range(1, nz):
            at = slice(j * LANE, (j + 1) * LANE)
            line = line + hid[0, mine, at].astype(F32) + hid[1, mine, at].astype(F32)
        wide = jnp.concatenate([line] + [jnp.zeros_like(line)] * (width // LANE - 1), axis=1)
        last = (iota((crows, width), 0) & (BLK - 1)) == BLK - 1
        out = jnp.where(last, wide, grad).astype(BF)
        rgrad[mine, :] = out
        if k == 0:
            back[0:BLK, :] = out[0:BLK]

        @pl.loop(max(1, k * per), (k + 1) * per)
        def _(q):
            ret_copy(q).start()

    stages = [arrive, partials]
    stages += [functools.partial(lambda k, h: rs_hop(k, h), h=h) for h in range(1, ha)]
    stages += [swiglu]
    stages += [functools.partial(lambda k, h: ag_hop(k, h), h=h) for h in range(ha)]
    stages += [give_back]
    for tick in range(len(stages) + chunks - 1):
        for k in range(chunks):
            if 0 <= tick - k < len(stages):
                stages[tick - k](k)

    xs, gs, col = split_rows(recv[...], width)
    scaled = (gs.astype(F32) * col).astype(BF)
    ggrad_ref[...] = dot(xs, hid[1], 0, 0).astype(BF)
    store(0).start()
    ugrad_ref[...] = dot(xs, hid[2], 0, 0).astype(BF)
    store(1).start()
    dgrad_ref[...] = dot(hid[0], scaled, 0, 0).astype(BF)
    store(2).start()

    @pl.loop(1, slots)
    def _(q):
        ret_copy(q).wait_recv()

    picks = sel[slots : slots + toks, :]
    xgrad_ref[...] = dot(picks, back[...]).astype(BF)
    lines = back[...].astype(F32).reshape(slots, BLK, width)[:, BLK - 1, 0:LANE].astype(BF)
    line_x = jnp.where(own_lane, dot(lines, spread, 1, 1), 0.0)
    line_vec = jnp.sum(line_x, axis=0, keepdims=True)
    table = dot((picks.astype(F32) * line_vec).astype(BF), expand, 1, 1)
    result = jnp.zeros((toks, topk), F32)
    k_lane = iota((toks, topk), 1)
    for k in range(topk):
        hit = ids[:, k : k + 1] == named
        value = jnp.sum(jnp.where(hit, table, 0.0), axis=1, keepdims=True)
        result = jnp.where(k_lane == k, value, result)
    pgrad_ref[...] = dot(result.astype(BF), eye, 0, 0).astype(BF)

    for i in range(3):
        store(i).wait()
        w_copy(i).wait_send()

    @pl.loop(1, slots)
    def _(q):
        disp_copy(q).wait_send()
        ret_copy(q).wait_send()

    for k in range(chunks):
        fwd_copy(k).wait_send()
        for i in range(ha + hb):
            rs_copy(k, i).wait_send()
            ag_copy(k, i).wait_send()
        for j in range(nz):
            at = hid.at[:, half_rows(k, core), pl.ds(j * LANE, LANE)]
            remote(at, at, pt_s.at[k, j], pt_r.at[k, j], other).wait_send()


def copy_out(*refs):
    n = (len(refs) - 2) // 3
    srcs, dsts, held = refs[:n], refs[n : 2 * n], refs[2 * n : 3 * n]
    ins = [pltpu.make_async_copy(srcs[i], held[i], refs[3 * n].at[i]) for i in range(n)]
    outs = [pltpu.make_async_copy(held[i], dsts[i], refs[3 * n + 1].at[i]) for i in range(n)]
    for i in range(n):
        ins[i].start()
    for i in range(n):
        ins[i].wait()
        outs[i].start()
    for i in range(n):
        outs[i].wait()


def on_device(sizes, layer_input, output_grad, route_ids, route_probs, gate_weight, up_weight, down_weight):
    nx, ny, nz = sizes
    toks, width = layer_input.shape
    hidden = gate_weight.shape[2]
    topk = route_ids.shape[1]
    slots = nx * ny
    rows = slots * BLK
    chunks = ny // 2
    half = nx * BLK
    hops = nz - 1
    assert hidden == nz * LANE
    assert 3 * toks * topk // (2 * slots) < BLK
    vmem = pl.BlockSpec(memory_space=pltpu.VMEM)
    anyw = pl.BlockSpec(memory_space=pl.ANY)
    dma = pltpu.SemaphoreType.DMA
    out_shape = (
        jax.ShapeDtypeStruct((toks, width), BF),
        jax.ShapeDtypeStruct((topk, toks), BF),
        jax.ShapeDtypeStruct((width, hidden), BF),
        jax.ShapeDtypeStruct((width, hidden), BF),
        jax.ShapeDtypeStruct((hidden, width), BF),
    )
    outs = pl.pallas_call(
        functools.partial(kernel, nx, ny, nz),
        out_shape=out_shape,
        in_specs=[vmem] * 4 + [anyw] * 3,
        out_specs=[vmem] * 2 + [anyw] * 3,
        scratch_shapes=[
            pltpu.VMEM((slots + toks, 2 * width), BF),
            pltpu.VMEM((slots + toks, rows), BF),
            pltpu.VMEM((rows, 2 * width), BF),
            pltpu.VMEM((rows, 2 * width), BF),
            pltpu.VMEM((chunks, half, 2 * width), BF),
            pltpu.VMEM((chunks, 3, half, hidden), F32),
            pltpu.VMEM((chunks, hops, 3, half, LANE), BF),
            pltpu.VMEM((chunks, hops, 3, half, LANE), BF),
            pltpu.VMEM((3, rows, hidden), BF),
            pltpu.VMEM((rows, width), BF),
            pltpu.VMEM((rows, width), BF),
            pltpu.VMEM((width, hidden), BF),
            pltpu.VMEM((width, hidden), BF),
            pltpu.VMEM((hidden, width), BF),
            pltpu.VMEM((chunks, half, LANE), F32),
            pltpu.VMEM((width, hidden), BF),
            pltpu.VMEM((width, hidden), BF),
            pltpu.VMEM((hidden, width), BF),
            pltpu.VMEM((width, hidden), BF),
            pltpu.VMEM((width, hidden), BF),
            pltpu.VMEM((hidden, width), BF),
            dma((3,)), dma((3,)),
            dma((slots,)), dma((slots,)), dma((slots,)), dma((slots,)),
            dma((3,)), dma((3,)),
            dma((chunks,)), dma((chunks,)),
            dma((chunks, hops)), dma((chunks, hops)),
            dma((chunks, hops)), dma((chunks, hops)),
            dma((chunks, nz)), dma((chunks, nz)),
        ],
        compiler_params=pltpu.CompilerParams(
            collective_id=0, has_side_effects=True, vmem_limit_bytes=60 * 1024 * 1024
        ),
    )(
        layer_input, output_grad, route_ids.T, route_probs.T,
        gate_weight[0], up_weight[0], down_weight[0],
    )
    xgrad, pgrad, ggrad, ugrad, dgrad = pl.pallas_call(
        copy_out,
        out_shape=out_shape,
        in_specs=[anyw] * 5,
        out_specs=[anyw] * 5,
        scratch_shapes=[pltpu.VMEM(o.shape, o.dtype) for o in out_shape] + [dma((5,)), dma((5,))],
    )(*outs)
    return (xgrad, pgrad.T, ggrad[None], ugrad[None], dgrad[None])


def solution(mesh, sizes=(4, 8, 8)):
    placed = (
        P("expert", "dp"),
        P("expert", "dp"),
        P("expert", None),
        P("expert", None),
        P("expert", "dp", None),
        P("expert", "dp", None),
        P("expert", None, "dp"),
    )
    return jax.shard_map(
        functools.partial(on_device, sizes),
        mesh=mesh,
        in_specs=placed,
        out_specs=(
            P("expert", "dp"),
            P("expert", None),
            P("expert", "dp", None),
            P("expert", "dp", None),
            P("expert", None, "dp"),
        ),
        check_vma=False,
    )
```
